32 devices in a mesh: chan: 8 (over z, core), tm: 4 (over y, x).
Axes of the slice: x: 2, y: 2, z: 4, core: 2. Of those that a mesh axis runs over, the one named last changes fastest.
Arguments:
- spectra: bfloat16 [4, 1024, 1024], P('tm', 'chan')
- tile_bin: int32 [32], P('chan'), may hold values from 0 to 7
- owner_bins: int32 [8], replicated, may hold values from 0 to 7, each once
- source_slab: int32 [1], replicated, may hold values from 0 to 255
Outputs:
- stacks: float32 [8, 128, 512], P('chan', 'tm')
The draws below stay inside these ranges and needn't reach their ends.
Inputs may be any that keep to these rules, and one draw needn't show every extreme that they name: `tile_bin`: a tile of 128 pairs belongs to exactly one offset bin. `owner_bins`: every bin stands once. `source_slab`: the slab's 4 channels lie within one chan index's block.
All inputs are finite; a program needn't handle non-finite values.
Results may differ from the reference program's by a relative error of at most 0.005.
Values may be sent and summed in bfloat16 or wider, within the bound.
A program may use at most 64 MiB of HBM per device.

```python
import math
import jax
import jax.numpy as jnp
from jax import lax

CH_DEV = 128
NF = 512
LAGS = 512
SEG_LEN = 15000
K0 = 60
GROUP = 64
SRC = 4
PAIRS = 128
TILES = 32
CHANNELS = 1024
NBINS = 8
SEGMENTS = 4
N_CHAN = 8


def draw_spectra(key, part):
    base_key, chan_key, group_key = jax.random.split(key, 3)
    full_shape = (SEGMENTS, CHANNELS, 2 * NF)
    base = jax.random.normal(base_key, full_shape, jnp.float32)
    chan_scale = jnp.exp(jax.random.uniform(chan_key, (SEGMENTS, CHANNELS, 1, 1), jnp.float32) * 2.302585)
    group_scale = jnp.exp(jax.random.uniform(group_key, (SEGMENTS, CHANNELS, 1, NF // GROUP), jnp.float32) * 2.302585)
    grouped = base.reshape(SEGMENTS, CHANNELS, 2, NF // GROUP, GROUP) * (chan_scale * group_scale)[..., None]
    return grouped.reshape(full_shape).astype(jnp.bfloat16)


def with_ends(values, key, low, largest):
    dims = values.shape
    index_at = [jax.random.randint(jax.random.fold_in(key, axis), (), 0, dims[axis]) for axis in range(len(dims))]
    values = values.at[tuple(index_at)].set(low)
    longest = dims.index(max(dims))
    index_at[longest] = (index_at[longest] + 1) % dims[longest]
    return values.at[tuple(index_at)].set(largest)


def setup_inputs(seed: int = 0) -> dict:
    key_list = jax.random.split(jax.random.key(seed), 5)
    return {
        "spectra": draw_spectra(jax.random.fold_in(key_list[4], 71), 0),
        "tile_bin": with_ends(jax.random.randint(key_list[1], (TILES,), 0, NBINS), jax.random.fold_in(key_list[1], 1), 0, NBINS - 1).astype(jnp.int32),
        "owner_bins": jax.random.permutation(key_list[2], NBINS).astype(jnp.int32),
        "source_slab": jax.random.randint(key_list[3], (1,), 0, CHANNELS // SRC).astype(jnp.int32),
    }


def whiten_block(raw_block):
    values = raw_block.astype(jnp.float32)
    channels = values.shape[0]
    bands = values.shape[1] // 2
    grouped = values.reshape(channels, 2, bands // GROUP, GROUP)
    power = lax.optimization_barrier(jnp.mean(grouped[:, 0] * grouped[:, 0] + grouped[:, 1] * grouped[:, 1], axis=-1))
    inverse = 1.0 / jnp.sqrt(power + 1e-06)
    return (grouped * inverse[:, None, :, None]).reshape(channels, 2 * bands).astype(jnp.bfloat16)

def phase_tables(bands, lag_count):
    freq_index = (K0 + jnp.arange(bands)).astype(jnp.int32)
    lag_index = (jnp.arange(lag_count) - lag_count // 2).astype(jnp.int32)
    phase = freq_index[:, None] * lag_index[None, :] % SEG_LEN
    angle = phase.astype(jnp.float32) * (2.0 * math.pi / SEG_LEN)
    return (jnp.cos(angle), jnp.sin(angle))

def modulate(slab_rows, cosines, sines):
    values = slab_rows.astype(jnp.float32)
    bands = cosines.shape[0]
    real_part = values[:, :bands, None]
    imag_part = values[:, bands:, None]
    upper = real_part * cosines[None] + imag_part * sines[None]
    lower = imag_part * cosines[None] - real_part * sines[None]
    return jnp.concatenate([upper, lower], axis=1).astype(jnp.bfloat16)

def normalize(correlation):
    energy = lax.optimization_barrier(jnp.mean(correlation * correlation, axis=-1, keepdims=True))
    return correlation / jnp.sqrt(energy + 1e-06)

def reference(spectra, tile_bin, owner_bins, source_slab):
    cosines, sines = phase_tables(NF, LAGS)
    membership = (owner_bins[:, None] == tile_bin[None, :]).astype(jnp.float32)
    first_row = (source_slab[0] * SRC).astype(jnp.int32)

    def one_segment(total, raw_block):
        whitened = whiten_block(raw_block)
        slab_rows = lax.dynamic_slice_in_dim(whitened, first_row, SRC, 0)
        modulated = modulate(slab_rows, cosines, sines)
        correlation = jnp.einsum('ck,ikl->icl', whitened.astype(jnp.float32), modulated.astype(jnp.float32), precision=lax.Precision.HIGHEST)
        traces = normalize(correlation)
        tiles = traces.reshape(SRC, N_CHAN, CH_DEV // PAIRS, PAIRS, LAGS).transpose(1, 0, 2, 3, 4).reshape(TILES, PAIRS, LAGS)
        binned = jnp.einsum('rt,tpl->rpl', membership, tiles, precision=lax.Precision.HIGHEST)
        return (total + binned, None)
    total, _ = lax.scan(one_segment, jnp.zeros((NBINS, PAIRS, LAGS), jnp.float32), spectra)
    return total / SEGMENTS
```

```python
import functools
import math

import jax
import jax.numpy as jnp
import numpy as np
from jax import lax
from jax.experimental import pallas as pl
from jax.experimental.pallas import tpu as pltpu
from jax.sharding import PartitionSpec as P

LAGS = 512
SEG_LEN = 15000
K0 = 60
GROUP = 64
SRC = 4
PAIRS = 128
WIDE = 256
CHUNKS = 2
MESH = pl.DeviceIdType.MESH


def phase_table(bands):
    phase = (K0 + np.arange(bands))[:, None] * (np.arange(LAGS) - LAGS // 2)[None, :] % SEG_LEN
    angle = phase.astype(np.float64) * (2.0 * math.pi / SEG_LEN)
    return jnp.asarray(np.concatenate([np.cos(angle), np.sin(angle)]), dtype=jnp.bfloat16)


def whiten(real_part, imag_part, same_group):
    power = (real_part * real_part + imag_part * imag_part) * (1.0 / GROUP)
    high = power.astype(jnp.bfloat16)
    low = (power - high.astype(jnp.float32)).astype(jnp.bfloat16)
    mean = jnp.dot(high, same_group, preferred_element_type=jnp.float32)
    mean = mean + jnp.dot(low, same_group, preferred_element_type=jnp.float32)
    inverse = lax.rsqrt(mean + 1e-06)
    return [
        (part * inverse).astype(jnp.bfloat16).astype(jnp.float32)
        for part in (real_part, imag_part)
    ]


def kernel(
    n_chan, n_tm, tile_bin, owner_bins, source_slab, spectra, table_in, out,
    block, table, white, slabs, own, t_out, t_in, c_out, c_in,
    local_sems, s_send, s_recv, t_send, t_recv, c_send, c_recv,
):
    channels, columns = block.shape
    bands = columns // 2
    halves = bands // WIDE
    rows = channels // n_tm
    width = LAGS // CHUNKS
    chan = lax.axis_index("chan")
    tm = lax.axis_index("tm")
    near = 1
    while near * near * 4 <= n_tm:
        near *= 2
    near = n_tm // near
    tm_peer = []
    for off in range(n_tm):
        far_step, near_step = off // near, off % near
        far_at = lax.rem(tm // near + far_step, n_tm // near)
        tm_peer.append(far_at * near + lax.rem(lax.rem(tm, near) + near_step, near))
    chan_peer = [lax.rem(chan + off, n_chan) for off in range(n_chan)]

    barrier = pltpu.get_barrier_semaphore()
    for off in range(1, n_chan):
        pl.semaphore_signal(barrier, inc=1, device_id=(chan_peer[off], tm), device_id_type=MESH)
    for off in range(1, n_tm):
        pl.semaphore_signal(barrier, inc=1, device_id=(chan, tm_peer[off]), device_id_type=MESH)
    load_block = pltpu.make_async_copy(spectra.at[0], block, local_sems.at[0])
    load_table = pltpu.make_async_copy(table_in, table, local_sems.at[1])
    load_block.start()
    load_table.start()

    slab = source_slab[0]
    slabs_per_block = channels // SRC
    root = slab // slabs_per_block
    first_row = lax.rem(slab, slabs_per_block) * SRC
    blocks = columns // WIDE
    pick_row = lax.broadcasted_iota(jnp.int32, (SRC * blocks, channels), 0)
    pick_col = lax.broadcasted_iota(jnp.int32, (SRC * blocks, channels), 1)
    same_group = (
        lax.broadcasted_iota(jnp.int32, (WIDE, WIDE), 0) // GROUP
        == lax.broadcasted_iota(jnp.int32, (WIDE, WIDE), 1) // GROUP
    )
    same_group = jnp.where(same_group, 1.0, 0.0).astype(jnp.bfloat16)

    load_block.wait()
    picked = jnp.zeros((SRC * blocks, WIDE), jnp.float32)
    for c in range(blocks):
        chosen = pick_row - SRC * c == pick_col - first_row
        chosen = chosen & (pick_row >= SRC * c) & (pick_row < SRC * (c + 1))
        picked = picked + jnp.dot(
            jnp.where(chosen, 1.0, 0.0).astype(jnp.bfloat16),
            block[:, c * WIDE : (c + 1) * WIDE],
            preferred_element_type=jnp.float32,
        )
    slabs[0] = picked.astype(jnp.bfloat16)
    pl.semaphore_wait(barrier, n_chan + n_tm - 2)
    slab_copies = []
    for off in range(1, n_chan):
        copy = pltpu.make_async_remote_copy(
            src_ref=slabs.at[0],
            dst_ref=slabs.at[off],
            send_sem=s_send.at[off - 1],
            recv_sem=s_recv.at[off - 1],
            device_id=(chan_peer[off], tm),
            device_id_type=MESH,
        )
        copy.start()
        slab_copies.append(copy)

    for h in range(halves):
        real_at = slice(h * WIDE, (h + 1) * WIDE)
        imag_at = slice(bands + h * WIDE, bands + (h + 1) * WIDE)
        white[:, real_at], white[:, imag_at] = whiten(
            block[:, real_at].astype(jnp.float32),
            block[:, imag_at].astype(jnp.float32),
            same_group,
        )
    for copy in slab_copies:
        copy.wait_recv()
    source = slabs[lax.rem(chan - root + n_chan, n_chan)].astype(jnp.float32)
    source_real, source_imag = whiten(
        source[: SRC * halves], source[SRC * halves :], same_group
    )
    load_table.wait()

    t_copies = [[] for _ in range(CHUNKS)]
    for off in [*reversed(range(1, n_tm)), 0]:
        at = pl.ds(pl.multiple_of(tm_peer[off] * rows, rows), rows)
        products = []
        for i in range(SRC):
            upper, lower = [], []
            for h in range(halves):
                a = white[at, h * WIDE : (h + 1) * WIDE]
                b = white[at, bands + h * WIDE : bands + (h + 1) * WIDE]
                c = source_real[h * SRC + i : h * SRC + i + 1]
                d = source_imag[h * SRC + i : h * SRC + i + 1]
                upper.append(a * c + b * d)
                lower.append(a * d - b * c)
            products.append(jnp.concatenate(upper + lower, axis=1))
        product = jnp.concatenate(products, axis=0).astype(jnp.bfloat16)
        correlation = jnp.dot(product, table[...], preferred_element_type=jnp.float32)
        energy = jnp.mean(correlation * correlation, axis=-1, keepdims=True)
        traces = correlation * (lax.rsqrt(energy + 1e-06) * (1.0 / n_tm))
        if off == 0:
            own[...] = traces
            continue
        for h in range(CHUNKS):
            t_out[off - 1, h] = traces[:, h * width : (h + 1) * width].astype(jnp.bfloat16)
            copy = pltpu.make_async_remote_copy(
                src_ref=t_out.at[off - 1, h],
                dst_ref=t_in.at[off - 1, h],
                send_sem=t_send.at[off - 1, h],
                recv_sem=t_recv.at[off - 1, h],
                device_id=(chan, tm_peer[off]),
                device_id_type=MESH,
            )
            copy.start()
            t_copies[h].append(copy)

    c_copies = [[] for _ in range(CHUNKS)]
    for h in range(CHUNKS):
        summed = own[:, h * width : (h + 1) * width]
        for n, copy in enumerate(t_copies[h]):
            copy.wait_recv()
            summed = summed + t_in[n_tm - 2 - n, h].astype(jnp.float32)
        for off in [*range(1, n_chan), 0]:
            bin_here = owner_bins[chan_peer[off]]
            binned = jnp.zeros((rows, width), jnp.float32)
            for i in range(SRC):
                member = jnp.where(tile_bin[i] == bin_here, 1.0, 0.0)
                binned = binned + summed[i * rows : (i + 1) * rows] * member
            if off == 0:
                out[0, :, h * width : (h + 1) * width] = binned
                continue
            c_out[off - 1, h] = binned.astype(jnp.bfloat16)
            copy = pltpu.make_async_remote_copy(
                src_ref=c_out.at[off - 1, h],
                dst_ref=c_in.at[off - 1, h],
                send_sem=c_send.at[off - 1, h],
                recv_sem=c_recv.at[off - 1, h],
                device_id=(chan_peer[off], tm),
                device_id_type=MESH,
            )
            copy.start()
            c_copies[h].append(copy)
    for h in range(CHUNKS):
        total = out[0, :, h * width : (h + 1) * width]
        for n, copy in enumerate(c_copies[h]):
            copy.wait_recv()
            total = total + c_in[n, h].astype(jnp.float32)
        out[0, :, h * width : (h + 1) * width] = total
    for copy in slab_copies + sum(t_copies, []) + sum(c_copies, []):
        copy.wait_send()


def per_device(n_chan, n_tm, spectra, tile_bin, owner_bins, source_slab):
    _, channels, columns = spectra.shape
    rows = channels // n_tm
    width = LAGS // CHUNKS
    smem = pl.BlockSpec(memory_space=pltpu.SMEM)
    anywhere = pl.BlockSpec(memory_space=pl.ANY)
    dma = pltpu.SemaphoreType.DMA
    return pl.pallas_call(
        functools.partial(kernel, n_chan, n_tm),
        out_shape=jax.ShapeDtypeStruct((1, rows, LAGS), jnp.float32),
        in_specs=[smem, smem, smem, anywhere, anywhere],
        out_specs=pl.BlockSpec(memory_space=pltpu.VMEM),
        scratch_shapes=[
            pltpu.VMEM((channels, columns), jnp.bfloat16),
            pltpu.VMEM((columns, LAGS), jnp.bfloat16),
            pltpu.VMEM((channels, columns), jnp.float32),
            pltpu.VMEM((n_chan, SRC * columns // WIDE, WIDE), jnp.bfloat16),
            pltpu.VMEM((SRC * rows, LAGS), jnp.float32),
            pltpu.VMEM((n_tm - 1, CHUNKS, SRC * rows, width), jnp.bfloat16),
            pltpu.VMEM((n_tm - 1, CHUNKS, SRC * rows, width), jnp.bfloat16),
            pltpu.VMEM((n_chan - 1, CHUNKS, rows, width), jnp.bfloat16),
            pltpu.VMEM((n_chan - 1, CHUNKS, rows, width), jnp.bfloat16),
            dma((2,)),
            dma((n_chan - 1,)),
            dma((n_chan - 1,)),
            dma((n_tm - 1, CHUNKS)),
            dma((n_tm - 1, CHUNKS)),
            dma((n_chan - 1, CHUNKS)),
            dma((n_chan - 1, CHUNKS)),
        ],
        compiler_params=pltpu.CompilerParams(
            collective_id=0, has_side_effects=True, vmem_limit_bytes=32 * 1024 * 1024
        ),
        name="stack_kernel",
    )(tile_bin, owner_bins, source_slab, spectra, phase_table(columns // 2))


def solution(mesh):
    return jax.shard_map(
        functools.partial(per_device, mesh.shape["chan"], mesh.shape["tm"]),
        mesh=mesh,
        in_specs=(P("tm", "chan", None), P("chan"), P(), P()),
        out_specs=P("chan", "tm", None),
        check_vma=False,
    )
```

```python
import functools
import math

import jax
import jax.numpy as jnp
import numpy as np
from jax import lax
from jax.experimental import pallas as pl
from jax.experimental.pallas import tpu as pltpu
from jax.sharding import PartitionSpec as P

LAGS = 512
SEG_LEN = 15000
K0 = 60
GROUP = 64
SRC = 4
PAIRS = 128
WIDE = 256
CHUNKS = 2
MESH = pl.DeviceIdType.MESH


def phase_table(bands):
    phase = (K0 + np.arange(bands))[:, None] * (np.arange(LAGS) - LAGS // 2)[None, :] % SEG_LEN
    angle = phase.astype(np.float64) * (2.0 * math.pi / SEG_LEN)
    return jnp.asarray(np.concatenate([np.cos(angle), np.sin(angle)]), dtype=jnp.bfloat16)


def whiten(real_part, imag_part, same_group):
    power = (real_part * real_part + imag_part * imag_part) * (1.0 / GROUP)
    high = power.astype(jnp.bfloat16)
    low = (power - high.astype(jnp.float32)).astype(jnp.bfloat16)
    mean = jnp.dot(high, same_group, preferred_element_type=jnp.float32)
    mean = mean + jnp.dot(low, same_group, preferred_element_type=jnp.float32)
    inverse = lax.rsqrt(mean + 1e-06)
    return [
        (part * inverse).astype(jnp.bfloat16).astype(jnp.float32)
        for part in (real_part, imag_part)
    ]


def kernel(
    n_chan, n_tm, tile_in, owner_in, slab_in, spectra, table_in, out,
    tile_bin, owner_bins, source_slab, block, table, white, slabs, own, t_out, t_in, c_out, c_in,
    local_sems, s_send, s_recv, t_send, t_recv, c_send, c_recv,
):
    channels, columns = block.shape
    bands = columns // 2
    halves = bands // WIDE
    rows = channels // n_tm
    width = LAGS // CHUNKS
    chan = lax.axis_index("chan")
    tm = lax.axis_index("tm")
    near = 1
    while near * near * 4 <= n_tm:
        near *= 2
    near = n_tm // near
    tm_peer = []
    for off in range(n_tm):
        far_step, near_step = off // near, off % near
        far_at = lax.rem(tm // near + far_step, n_tm // near)
        tm_peer.append(far_at * near + lax.rem(lax.rem(tm, near) + near_step, near))
    chan_peer = [lax.rem(chan + off, n_chan) for off in range(n_chan)]

    barrier = pltpu.get_barrier_semaphore()
    for off in range(1, n_chan):
        pl.semaphore_signal(barrier, inc=1, device_id=(chan_peer[off], tm), device_id_type=MESH)
    for off in range(1, n_tm):
        pl.semaphore_signal(barrier, inc=1, device_id=(chan, tm_peer[off]), device_id_type=MESH)
    load_block = pltpu.make_async_copy(spectra.at[0], block, local_sems.at[0])
    load_table = pltpu.make_async_copy(table_in, table, local_sems.at[1])
    load_slab = pltpu.make_async_copy(slab_in, source_slab, local_sems.at[2])
    load_tiles = pltpu.make_async_copy(tile_in, tile_bin, local_sems.at[3])
    load_owners = pltpu.make_async_copy(owner_in, owner_bins, local_sems.at[4])
    for load in (load_slab, load_block, load_tiles, load_owners, load_table):
        load.start()

    load_slab.wait()
    slab = source_slab[0]
    slabs_per_block = channels // SRC
    root = slab // slabs_per_block
    first_row = lax.rem(slab, slabs_per_block) * SRC
    blocks = columns // WIDE
    pick_row = lax.broadcasted_iota(jnp.int32, (SRC * blocks, channels), 0)
    pick_col = lax.broadcasted_iota(jnp.int32, (SRC * blocks, channels), 1)
    same_group = (
        lax.broadcasted_iota(jnp.int32, (WIDE, WIDE), 0) // GROUP
        == lax.broadcasted_iota(jnp.int32, (WIDE, WIDE), 1) // GROUP
    )
    same_group = jnp.where(same_group, 1.0, 0.0).astype(jnp.bfloat16)

    load_block.wait()
    picked = jnp.zeros((SRC * blocks, WIDE), jnp.float32)
    for c in range(blocks):
        chosen = pick_row - SRC * c == pick_col - first_row
        chosen = chosen & (pick_row >= SRC * c) & (pick_row < SRC * (c + 1))
        picked = picked + jnp.dot(
            jnp.where(chosen, 1.0, 0.0).astype(jnp.bfloat16),
            block[:, c * WIDE : (c + 1) * WIDE],
            preferred_element_type=jnp.float32,
        )
    slabs[0] = picked.astype(jnp.bfloat16)
    pl.semaphore_wait(barrier, n_chan + n_tm - 2)
    slab_copies = []
    for off in range(1, n_chan):
        copy = pltpu.make_async_remote_copy(
            src_ref=slabs.at[0],
            dst_ref=slabs.at[off],
            send_sem=s_send.at[off - 1],
            recv_sem=s_recv.at[off - 1],
            device_id=(chan_peer[off], tm),
            device_id_type=MESH,
        )
        copy.start()
        slab_copies.append(copy)

    for h in range(halves):
        real_at = slice(h * WIDE, (h + 1) * WIDE)
        imag_at = slice(bands + h * WIDE, bands + (h + 1) * WIDE)
        white[:, real_at], white[:, imag_at] = whiten(
            block[:, real_at].astype(jnp.float32),
            block[:, imag_at].astype(jnp.float32),
            same_group,
        )
    for copy in slab_copies:
        copy.wait_recv()
    source = slabs[lax.rem(chan - root + n_chan, n_chan)].astype(jnp.float32)
    source_real, source_imag = whiten(
        source[: SRC * halves], source[SRC * halves :], same_group
    )
    for load in (load_tiles, load_owners, load_table):
        load.wait()

    t_copies = [[] for _ in range(CHUNKS)]
    for off in [*reversed(range(1, n_tm)), 0]:
        at = pl.ds(pl.multiple_of(tm_peer[off] * rows, rows), rows)
        products = []
        for i in range(SRC):
            upper, lower = [], []
            for h in range(halves):
                a = white[at, h * WIDE : (h + 1) * WIDE]
                b = white[at, bands + h * WIDE : bands + (h + 1) * WIDE]
                c = source_real[h * SRC + i : h * SRC + i + 1]
                d = source_imag[h * SRC + i : h * SRC + i + 1]
                upper.append(a * c + b * d)
                lower.append(a * d - b * c)
            products.append(jnp.concatenate(upper + lower, axis=1))
        product = jnp.concatenate(products, axis=0).astype(jnp.bfloat16)
        correlation = jnp.dot(product, table[...], preferred_element_type=jnp.float32)
        energy = jnp.mean(correlation * correlation, axis=-1, keepdims=True)
        traces = correlation * (lax.rsqrt(energy + 1e-06) * (1.0 / n_tm))
        if off == 0:
            own[...] = traces
            continue
        for h in range(CHUNKS):
            t_out[off - 1, h] = traces[:, h * width : (h + 1) * width].astype(jnp.bfloat16)
            copy = pltpu.make_async_remote_copy(
                src_ref=t_out.at[off - 1, h],
                dst_ref=t_in.at[off - 1, h],
                send_sem=t_send.at[off - 1, h],
                recv_sem=t_recv.at[off - 1, h],
                device_id=(chan, tm_peer[off]),
                device_id_type=MESH,
            )
            t_copies[h].append(copy)

    for copy in sum(t_copies, []):
        copy.start()

    c_copies = [[] for _ in range(CHUNKS)]
    for h in range(CHUNKS):
        summed = own[:, h * width : (h + 1) * width]
        for n, copy in enumerate(t_copies[h]):
            copy.wait_recv()
            summed = summed + t_in[n_tm - 2 - n, h].astype(jnp.float32)
        for off in [*range(1, n_chan), 0]:
            bin_here = owner_bins[chan_peer[off]]
            binned = jnp.zeros((rows, width), jnp.float32)
            for i in range(SRC):
                member = jnp.where(tile_bin[i] == bin_here, 1.0, 0.0)
                binned = binned + summed[i * rows : (i + 1) * rows] * member
            if off == 0:
                out[0, :, h * width : (h + 1) * width] = binned
                continue
            c_out[off - 1, h] = binned.astype(jnp.bfloat16)
            copy = pltpu.make_async_remote_copy(
                src_ref=c_out.at[off - 1, h],
                dst_ref=c_in.at[off - 1, h],
                send_sem=c_send.at[off - 1, h],
                recv_sem=c_recv.at[off - 1, h],
                device_id=(chan_peer[off], tm),
                device_id_type=MESH,
            )
            copy.start()
            c_copies[h].append(copy)
    for h in range(CHUNKS):
        total = out[0, :, h * width : (h + 1) * width]
        for n, copy in enumerate(c_copies[h]):
            copy.wait_recv()
            total = total + c_in[n, h].astype(jnp.float32)
        out[0, :, h * width : (h + 1) * width] = total
    for copy in slab_copies + sum(t_copies, []) + sum(c_copies, []):
        copy.wait_send()


def per_device(n_chan, n_tm, spectra, tile_bin, owner_bins, source_slab):
    _, channels, columns = spectra.shape
    rows = channels // n_tm
    width = LAGS // CHUNKS
    in_place = pl.BlockSpec(memory_space=pltpu.HBM)
    dma = pltpu.SemaphoreType.DMA
    return pl.pallas_call(
        functools.partial(kernel, n_chan, n_tm),
        out_shape=jax.ShapeDtypeStruct((1, rows, LAGS), jnp.float32),
        in_specs=[in_place] * 5,
        out_specs=pl.BlockSpec(memory_space=pltpu.VMEM),
        scratch_shapes=[
            pltpu.SMEM(tile_bin.shape, jnp.int32),
            pltpu.SMEM(owner_bins.shape, jnp.int32),
            pltpu.SMEM(source_slab.shape, jnp.int32),
            pltpu.VMEM((channels, columns), jnp.bfloat16),
            pltpu.VMEM((columns, LAGS), jnp.bfloat16),
            pltpu.VMEM((channels, columns), jnp.float32),
            pltpu.VMEM((n_chan, SRC * columns // WIDE, WIDE), jnp.bfloat16),
            pltpu.VMEM((SRC * rows, LAGS), jnp.float32),
            pltpu.VMEM((n_tm - 1, CHUNKS, SRC * rows, width), jnp.bfloat16),
            pltpu.VMEM((n_tm - 1, CHUNKS, SRC * rows, width), jnp.bfloat16),
            pltpu.VMEM((n_chan - 1, CHUNKS, rows, width), jnp.bfloat16),
            pltpu.VMEM((n_chan - 1, CHUNKS, rows, width), jnp.bfloat16),
            dma((5,)),
            dma((n_chan - 1,)),
            dma((n_chan - 1,)),
            dma((n_tm - 1, CHUNKS)),
            dma((n_tm - 1, CHUNKS)),
            dma((n_chan - 1, CHUNKS)),
            dma((n_chan - 1, CHUNKS)),
        ],
        compiler_params=pltpu.CompilerParams(
            collective_id=0, has_side_effects=True, vmem_limit_bytes=55040 * 1024
        ),
        name="stack_kernel",
    )(tile_bin, owner_bins, source_slab, spectra, phase_table(columns // 2))


def solution(mesh):
    return jax.shard_map(
        functools.partial(per_device, mesh.shape["chan"], mesh.shape["tm"]),
        mesh=mesh,
        in_specs=(P("tm", "chan", None), P("chan"), P(), P()),
        out_specs=P("chan", "tm", None),
        check_vma=False,
    )
```

```python
import functools
import math

import jax
import jax.numpy as jnp
import numpy as np
from jax import lax
from jax.experimental import pallas as pl
from jax.experimental.pallas import tpu as pltpu
from jax.sharding import PartitionSpec as P

LAGS = 512
SEG_LEN = 15000
K0 = 60
GROUP = 64
SRC = 4
PAIRS = 128
WIDE = 256
RANK = 128
MESH = pl.DeviceIdType.MESH


def phase_factors(bands):
    lag_index = np.arange(LAGS) - LAGS // 2
    phase = (K0 + np.arange(bands))[:, None] * lag_index[None, :] % SEG_LEN
    angle = phase.astype(np.float64) * (2.0 * math.pi / SEG_LEN)
    waves = np.concatenate([np.cos(angle), np.sin(angle)])
    grid = (lag_index + 0.5) / (LAGS / 2)
    basis = np.full((1, LAGS), LAGS**-0.5)
    while len(basis) < RANK:
        row = grid * basis[-1]
        for _ in range(2):
            row = row - np.sum(np.sum(basis * row, axis=1, keepdims=True) * basis, axis=0)
        basis = np.concatenate([basis, row[None] / np.sqrt(np.sum(row * row))])
    factor = waves @ basis.T
    assert np.abs(factor @ basis - waves).max() < 1e-9
    return jnp.asarray(factor, jnp.bfloat16), jnp.asarray(basis, jnp.float32)


def whiten(real_part, imag_part, same_group):
    power = (real_part * real_part + imag_part * imag_part) * (1.0 / GROUP)
    high = power.astype(jnp.bfloat16)
    low = (power - high.astype(jnp.float32)).astype(jnp.bfloat16)
    mean = jnp.dot(high, same_group, preferred_element_type=jnp.float32)
    mean = mean + jnp.dot(low, same_group, preferred_element_type=jnp.float32)
    inverse = lax.rsqrt(mean + 1e-06)
    return [
        (part * inverse).astype(jnp.bfloat16).astype(jnp.float32)
        for part in (real_part, imag_part)
    ]


def kernel(
    n_chan, n_tm, tile_in, owner_in, slab_in, spectra, table_in, basis_in, out,
    tile_bin, owner_bins, source_slab, block, table, basis, white, slabs, own, t_out, t_in, c_out, c_in,
    local_sems, s_send, s_recv, t_send, t_recv, c_send, c_recv,
):
    channels, columns = block.shape
    bands = columns // 2
    halves = bands // WIDE
    rows = channels // n_tm
    chan = lax.axis_index("chan")
    tm = lax.axis_index("tm")
    near = 1
    while near * near * 4 <= n_tm:
        near *= 2
    near = n_tm // near
    tm_peer = []
    for off in range(n_tm):
        far_step, near_step = off // near, off % near
        far_at = lax.rem(tm // near + far_step, n_tm // near)
        tm_peer.append(far_at * near + lax.rem(lax.rem(tm, near) + near_step, near))
    chan_peer = [lax.rem(chan + off, n_chan) for off in range(n_chan)]

    barrier = pltpu.get_barrier_semaphore()
    for off in range(1, n_chan):
        pl.semaphore_signal(barrier, inc=1, device_id=(chan_peer[off], tm), device_id_type=MESH)
    for off in range(1, n_tm):
        pl.semaphore_signal(barrier, inc=1, device_id=(chan, tm_peer[off]), device_id_type=MESH)
    load_block = pltpu.make_async_copy(spectra.at[0], block, local_sems.at[0])
    load_table = pltpu.make_async_copy(table_in, table, local_sems.at[1])
    load_slab = pltpu.make_async_copy(slab_in, source_slab, local_sems.at[2])
    load_tiles = pltpu.make_async_copy(tile_in, tile_bin, local_sems.at[3])
    load_owners = pltpu.make_async_copy(owner_in, owner_bins, local_sems.at[4])
    load_basis = pltpu.make_async_copy(basis_in, basis, local_sems.at[5])
    for load in (load_slab, load_block, load_tiles, load_owners, load_table, load_basis):
        load.start()

    load_slab.wait()
    slab = source_slab[0]
    slabs_per_block = channels // SRC
    root = slab // slabs_per_block
    first_row = lax.rem(slab, slabs_per_block) * SRC
    blocks = columns // WIDE
    pick_row = lax.broadcasted_iota(jnp.int32, (SRC * blocks, channels), 0)
    pick_col = lax.broadcasted_iota(jnp.int32, (SRC * blocks, channels), 1)
    same_group = (
        lax.broadcasted_iota(jnp.int32, (WIDE, WIDE), 0) // GROUP
        == lax.broadcasted_iota(jnp.int32, (WIDE, WIDE), 1) // GROUP
    )
    same_group = jnp.where(same_group, 1.0, 0.0).astype(jnp.bfloat16)

    load_block.wait()
    picked = jnp.zeros((SRC * blocks, WIDE), jnp.float32)
    for c in range(blocks):
        chosen = pick_row - SRC * c == pick_col - first_row
        chosen = chosen & (pick_row >= SRC * c) & (pick_row < SRC * (c + 1))
        picked = picked + jnp.dot(
            jnp.where(chosen, 1.0, 0.0).astype(jnp.bfloat16),
            block[:, c * WIDE : (c + 1) * WIDE],
            preferred_element_type=jnp.float32,
        )
    slabs[0] = picked.astype(jnp.bfloat16)
    pl.semaphore_wait(barrier, n_chan + n_tm - 2)
    slab_copies = []
    for off in range(1, n_chan):
        copy = pltpu.make_async_remote_copy(
            src_ref=slabs.at[0],
            dst_ref=slabs.at[off],
            send_sem=s_send.at[off - 1],
            recv_sem=s_recv.at[off - 1],
            device_id=(chan_peer[off], tm),
            device_id_type=MESH,
        )
        copy.start()
        slab_copies.append(copy)

    for h in range(halves):
        real_at = slice(h * WIDE, (h + 1) * WIDE)
        imag_at = slice(bands + h * WIDE, bands + (h + 1) * WIDE)
        white[:, real_at], white[:, imag_at] = whiten(
            block[:, real_at].astype(jnp.float32),
            block[:, imag_at].astype(jnp.float32),
            same_group,
        )
    for copy in slab_copies:
        copy.wait_recv()
    source = slabs[lax.rem(chan - root + n_chan, n_chan)].astype(jnp.float32)
    source_real, source_imag = whiten(
        source[: SRC * halves], source[SRC * halves :], same_group
    )
    for load in (load_tiles, load_owners, load_table):
        load.wait()

    t_copies = []
    for off in [*reversed(range(1, n_tm)), 0]:
        at = pl.ds(pl.multiple_of(tm_peer[off] * rows, rows), rows)
        products = []
        for i in range(SRC):
            upper, lower = [], []
            for h in range(halves):
                a = white[at, h * WIDE : (h + 1) * WIDE]
                b = white[at, bands + h * WIDE : bands + (h + 1) * WIDE]
                c = source_real[h * SRC + i : h * SRC + i + 1]
                d = source_imag[h * SRC + i : h * SRC + i + 1]
                upper.append(a * c + b * d)
                lower.append(a * d - b * c)
            products.append(jnp.concatenate(upper + lower, axis=1))
        product = jnp.concatenate(products, axis=0).astype(jnp.bfloat16)
        correlation = jnp.dot(product, table[...], preferred_element_type=jnp.float32)
        energy = jnp.sum(correlation * correlation, axis=-1, keepdims=True) * (1.0 / LAGS)
        traces = correlation * (lax.rsqrt(energy + 1e-06) * (1.0 / n_tm))
        if off == 0:
            own[...] = traces
            continue
        t_out[off - 1] = traces.astype(jnp.bfloat16)
        copy = pltpu.make_async_remote_copy(
            src_ref=t_out.at[off - 1],
            dst_ref=t_in.at[off - 1],
            send_sem=t_send.at[off - 1],
            recv_sem=t_recv.at[off - 1],
            device_id=(chan, tm_peer[off]),
            device_id_type=MESH,
        )
        copy.start()
        t_copies.append(copy)

    members = [
        [jnp.where(tile_bin[i] == owner_bins[peer], 1.0, 0.0) for i in range(SRC)]
        for peer in chan_peer
    ]
    summed = own[...]
    for n, copy in reversed([*enumerate(t_copies)]):
        copy.wait_recv()
        summed = summed + t_in[n_tm - 2 - n].astype(jnp.float32)
    c_copies = []
    for off in [*range(1, n_chan), 0]:
        binned = jnp.zeros((rows, RANK), jnp.float32)
        for i in range(SRC):
            binned = binned + summed[i * rows : (i + 1) * rows] * members[off][i]
        if off == 0:
            total = binned
            continue
        c_out[off - 1] = binned.astype(jnp.bfloat16)
        copy = pltpu.make_async_remote_copy(
            src_ref=c_out.at[off - 1],
            dst_ref=c_in.at[off - 1],
            send_sem=c_send.at[off - 1],
            recv_sem=c_recv.at[off - 1],
            device_id=(chan_peer[off], tm),
            device_id_type=MESH,
        )
        copy.start()
        c_copies.append(copy)
    load_basis.wait()
    for n, copy in enumerate(c_copies):
        copy.wait_recv()
        total = total + c_in[n].astype(jnp.float32)
    out[0] = jnp.dot(
        total, basis[...], precision=lax.Precision.HIGHEST, preferred_element_type=jnp.float32
    )
    for copy in slab_copies + t_copies + c_copies:
        copy.wait_send()


def per_device(n_chan, n_tm, spectra, tile_bin, owner_bins, source_slab):
    _, channels, columns = spectra.shape
    rows = channels // n_tm
    in_place = pl.BlockSpec(memory_space=pltpu.HBM)
    dma = pltpu.SemaphoreType.DMA
    return pl.pallas_call(
        functools.partial(kernel, n_chan, n_tm),
        out_shape=jax.ShapeDtypeStruct((1, rows, LAGS), jnp.float32),
        in_specs=[in_place] * 6,
        out_specs=pl.BlockSpec(memory_space=pltpu.VMEM),
        scratch_shapes=[
            pltpu.SMEM(tile_bin.shape, jnp.int32),
            pltpu.SMEM(owner_bins.shape, jnp.int32),
            pltpu.SMEM(source_slab.shape, jnp.int32),
            pltpu.VMEM((channels, columns), jnp.bfloat16),
            pltpu.VMEM((columns, RANK), jnp.bfloat16),
            pltpu.VMEM((RANK, LAGS), jnp.float32),
            pltpu.VMEM((channels, columns), jnp.float32),
            pltpu.VMEM((n_chan, SRC * columns // WIDE, WIDE), jnp.bfloat16),
            pltpu.VMEM((SRC * rows, RANK), jnp.float32),
            pltpu.VMEM((n_tm - 1, SRC * rows, RANK), jnp.bfloat16),
            pltpu.VMEM((n_tm - 1, SRC * rows, RANK), jnp.bfloat16),
            pltpu.VMEM((n_chan - 1, rows, RANK), jnp.bfloat16),
            pltpu.VMEM((n_chan - 1, rows, RANK), jnp.bfloat16),
            dma((6,)),
            dma((n_chan - 1,)),
            dma((n_chan - 1,)),
            dma((n_tm - 1,)),
            dma((n_tm - 1,)),
            dma((n_chan - 1,)),
            dma((n_chan - 1,)),
        ],
        compiler_params=pltpu.CompilerParams(
            collective_id=0, has_side_effects=True, vmem_limit_bytes=55040 * 1024
        ),
        name="stack_kernel",
    )(tile_bin, owner_bins, source_slab, spectra, *phase_factors(columns // 2))


def solution(mesh):
    return jax.shard_map(
        functools.partial(per_device, mesh.shape["chan"], mesh.shape["tm"]),
        mesh=mesh,
        in_specs=(P("tm", "chan", None), P("chan"), P(), P()),
        out_specs=P("chan", "tm", None),
        check_vma=False,
    )
```
